512 devices in a mesh: pipe: 8 (over x_hi, y), expert: 64 (over z, x_lo, core).
Axes of the slice: x: 4 (x_hi: 2, x_lo: 2; x = x_hi * 2 + x_lo), y: 4, z: 16, core: 2. Of those that a mesh axis runs over, the one named last changes fastest.
Arguments:
- activations: bfloat16 [8, 768, 3584], P('pipe', 'expert'), may hold values from -6 to 6
- out_grads: bfloat16 [8, 768, 3584], P('pipe', 'expert'), may hold values from -6 to 6
- gate_vals: float32 [8, 768, 8], P('pipe', 'expert'), may hold values from 0.05 to 0.3
- routes: int32 [8, 768, 8], P('pipe', 'expert'), may hold values from 0 to 15, all different within a row; in each aligned block of 12 rows (0 to 11, 12 to 23, ..., all dimensions but the last counted through in order) at most 9 rows name the same one
- up_weight: bfloat16 [8, 3584, 16384], P('pipe', None, 'expert'), may hold values from -0.09375 to 0.09375
- down_weight: bfloat16 [8, 16384, 3584], P('pipe', 'expert'), may hold values from -0.1875 to 0.1875
Outputs:
- handed_grads: bfloat16 [8, 768, 3584], P('pipe', 'expert')
- gate_grads: float32 [8, 768, 8], P('pipe', 'expert')
The draws below stay inside these ranges and needn't reach their ends.
Inputs may be any that keep to these rules, and one draw needn't show every extreme that they name: `routes`: each token names 8 different experts; among the 12 tokens of one device at most 9 name the same expert, and on some device some expert is named by exactly 9 of them.
All inputs are finite; a program needn't handle non-finite values.
Results may differ from the reference program's by a relative error of at most 0.008.
Values may be sent and summed in bfloat16 or wider, within the bound.
No kernel may reach another device: no remote copies, remote signals or barrier semaphores. Data moves between devices by JAX's collectives and lax.ppermute only.
A program may use at most 128 MiB of HBM per device.

```python
import math
import jax
import jax.numpy as jnp
import numpy as np
from jax import lax

D = 3584
HID = 1024
EXPERTS = 16
TOP = 8
TOK_DEV = 12
CAP = 9
SECTIONS = 8
TOKENS = 768


def block_levels(stream_key, extent, split, low, high):
    factor_of, own = 1.0, jax.random.fold_in(stream_key, 6)
    for axis_at, shards_of in split:
        draws = jnp.exp(jax.random.uniform(jax.random.fold_in(own, axis_at), (shards_of,), jnp.float32, low / len(split), high / len(split)))
        factor_of = factor_of * jnp.repeat(draws, extent[axis_at] // shards_of).reshape([-1 if axis == axis_at else 1 for axis in range(len(extent))])
    return factor_of


def assign_block(rng, own, number, rows, number_of, top, most, lean):
    order = jax.random.permutation(rng, number_of)
    crowded, usual = load_shares(number_of, rows * top, most, lean, True), load_shares(number_of, rows * top, most, lean, False)
    places = jnp.arange(number_of)

    def named(tallies, turn):
        used = int((tallies > 0).sum())
        fixed = max(1, used // 4)
        shifted = fixed + (places - fixed + turn * (used - fixed)) % max(1, number_of - fixed)
        return jnp.zeros((number_of,), jnp.int32).at[order[jnp.where(places < fixed, places, shifted)]].set(jnp.asarray(tallies, jnp.int32))

    tallies = jnp.where(number % 4 == 0, named(crowded, number // 4), named(usual, number - number // 4 - 1))
    mixed = jax.random.permutation(jax.random.fold_in(own, 3), number_of)
    donor, taker = mixed[0:number_of // 2 * 2:2], mixed[1:number_of // 2 * 2:2]
    margin = jnp.minimum(tallies[donor] - 1, most - tallies[taker]) // 2
    margin = jnp.where((donor == order[0]) | (taker == order[0]) | (tallies[taker] == 0), 0, jnp.maximum(margin, 0))
    shifted = jax.random.randint(jax.random.fold_in(own, 4), (number_of // 2,), 0, 1 << 20) % (margin + 1)
    tallies = tallies.at[donor].add(-shifted).at[taker].add(shifted)
    members = jnp.searchsorted(jnp.cumsum(tallies), jnp.arange(rows * top), side="right").astype(jnp.int32)
    grid = members.reshape(top, rows).T
    grid = grid[jax.random.permutation(jax.random.fold_in(own, 1), rows)]
    turn = jax.random.randint(jax.random.fold_in(own, 2), (rows, 1), 0, top)
    return jnp.take_along_axis(grid, (jnp.arange(top)[None, :] + turn) % top, axis=1)


def load_shares(count, total, reach, skew, full):
    portions = [(1 << 20) // math.isqrt(grade ** skew) + 1 for grade in range(1, count + 1)]
    largest = reach if full else min(reach, max(-(-total // count), total * portions[0] // sum(portions)))
    least = 1 if total - largest >= count - 1 else 0
    counts, rest = [largest] + [least] * (count - 1), total - largest - least * (count - 1)
    while rest > 0:
        candidates = [i for i in range(1, count) if counts[i] < largest] or [i for i in range(1, count) if counts[i] < reach]
        mass, left = sum([portions[i] for i in candidates]), rest
        for i in candidates:
            more = min(reach - counts[i], max(1, left * portions[i] // mass), rest)
            counts[i] = counts[i] + more
            rest = rest - more
    return np.array(counts)


def gaussian(own_key, shape, deviation, reach, pieces=(), kind=jnp.bfloat16):
    values = deviation * jax.random.normal(own_key, shape, jnp.float32)
    if pieces:
        values = values * block_levels(own_key, shape, pieces, -0.22, 0.18)
    return jnp.clip(values, -reach, reach).astype(kind)


def setup_inputs(seed: int = 0) -> dict:
    streams_of = jax.random.split(jax.random.key(seed), 7)
    activations = gaussian(streams_of[0], (SECTIONS, TOKENS, D), 1.0, 6.0, ((0, 8), (1, 64)))
    out_grads = gaussian(streams_of[1], (SECTIONS, TOKENS, D), 1.0, 6.0, ((0, 8), (1, 64)))
    gate_vals = jnp.clip(0.05 + 0.25 * jax.random.uniform(streams_of[2], (SECTIONS, TOKENS, TOP), jnp.float32) ** block_levels(streams_of[2], (SECTIONS, TOKENS, TOP), ((0, 8), (1, 64)), -0.2, 0.2), 0.05, 0.3)
    routes_keys = jax.random.split(jax.random.fold_in(streams_of[3], 1), SECTIONS * TOKENS // TOK_DEV)
    routes_turns = jax.random.permutation(jax.random.fold_in(streams_of[3], 3), SECTIONS * TOKENS // TOK_DEV)
    routes = jax.vmap(lambda own, number: assign_block(jax.random.fold_in(streams_of[3], 2), own, number, TOK_DEV, EXPERTS, TOP, CAP, 2))(routes_keys, routes_turns).reshape((SECTIONS, TOKENS, TOP))
    up_weight = gaussian(streams_of[4], (SECTIONS, D, EXPERTS * HID), D ** -0.5, 0.09375, ((0, 8), (2, 64)))
    down_weight = gaussian(streams_of[5], (SECTIONS, EXPERTS * HID, D), HID ** -0.5, 0.1875, ((0, 8), (1, 64)))
    return {"activations": activations, "out_grads": out_grads, "gate_vals": gate_vals, "routes": routes, "up_weight": up_weight, "down_weight": down_weight}


def silu_parts(pre_act):
    sig_val = jax.nn.sigmoid(pre_act)
    return pre_act * sig_val, sig_val * (1.0 + pre_act * (1.0 - sig_val))


def reference(activations, out_grads, gate_vals, routes, up_weight, down_weight):
    def one_section(index):
        inputs = activations[index]
        upstream = out_grads[index]
        section_gates = gate_vals[index]
        section_routes = routes[index]
        section_up = up_weight[index]
        section_down = down_weight[index]

        def per_expert(totals, expert_id):
            start_col = expert_id * HID
            up_cols = lax.dynamic_slice_in_dim(section_up, start_col, HID, 1)
            down_rows = lax.dynamic_slice_in_dim(section_down, start_col, HID, 0)
            pre_act = jnp.dot(inputs, up_cols, preferred_element_type=jnp.float32)
            hid_grad = jnp.dot(upstream, down_rows.T, preferred_element_type=jnp.float32)
            silu_val, silu_slope = silu_parts(pre_act)
            act_grad = (hid_grad * silu_slope).astype(jnp.bfloat16)
            expert_dx = jnp.dot(act_grad, up_cols.T, preferred_element_type=jnp.float32)
            expert_dg = jnp.sum(hid_grad * silu_val, axis=1)
            hit_mask = (section_routes == expert_id).astype(jnp.float32)
            grad_sum, gate_sum = totals
            grad_sum = grad_sum + jnp.sum(section_gates * hit_mask, axis=1)[:, None] * expert_dx
            gate_sum = gate_sum + hit_mask * expert_dg[:, None]
            return (grad_sum, gate_sum), expert_id

        start_vals = (jnp.zeros((TOKENS, D), jnp.float32), jnp.zeros((TOKENS, TOP), jnp.float32))
        finals, ignored = lax.scan(per_expert, start_vals, jnp.arange(EXPERTS, dtype=jnp.int32))
        return finals[0].astype(jnp.bfloat16), finals[1]

    input_grads, gate_grads = lax.map(one_section, jnp.arange(SECTIONS, dtype=jnp.int32))
    handed_grads = jnp.concatenate([input_grads[1:], jnp.zeros_like(input_grads[:1])], axis=0)
    return handed_grads, gate_grads
```

```python
import jax
import jax.numpy as jnp
from jax import lax
from jax.sharding import Mesh
from jax.sharding import PartitionSpec as P

EXPERTS = 16
COLUMN = ("z", "xl")
LANES = 128


def swap(block):
    return lax.ppermute(block, "c", [(0, 1), (1, 0)])


def pieces(values):
    high = values.astype(jnp.bfloat16)
    rest = values - high.astype(jnp.float32)
    middle = rest.astype(jnp.bfloat16)
    low = (rest - middle.astype(jnp.float32)).astype(jnp.bfloat16)
    return high, middle, low


def on_device(activations, out_grads, gate_vals, routes, up_weight, down_weight):
    inputs, upstream = activations[0], out_grads[0]
    gates, chosen = gate_vals[0], routes[0]
    local_up, local_down = up_weight[0], down_weight[0]
    tok, width = inputs.shape
    columns = lax.axis_size("z") * lax.axis_size("xl")
    core = lax.axis_index("c")
    first = core == 0
    expert = lax.axis_index("z")
    half = lax.axis_index("xl")

    onehot = (chosen[:, :, None] == jnp.arange(EXPERTS, dtype=jnp.int32)).astype(jnp.float32)
    dense = jnp.sum(onehot * gates[:, :, None], axis=1)
    tail = jnp.concatenate(pieces(dense), axis=1)
    tail = jnp.pad(tail, ((0, 0), (0, LANES - tail.shape[1])))

    keep = jnp.where(first, inputs, upstream)
    give = jnp.where(first, upstream, inputs)
    got = swap(jnp.concatenate([give, tail], axis=1))
    mine = jnp.concatenate([keep, tail], axis=1)
    block = jnp.concatenate([jnp.where(first, mine, got), jnp.where(first, got, mine)], axis=0)
    every = lax.all_gather(block, COLUMN, axis=0, tiled=True)

    up_rows = local_up.T
    other_up = swap(up_rows)
    both_up = jnp.concatenate(
        [jnp.where(first, up_rows, other_up), jnp.where(first, other_up, up_rows)], axis=0
    )
    other_down = lax.ppermute(local_down, "c", [(0, 1)])
    both_down = jnp.concatenate([other_down, local_down], axis=0)
    weights = jnp.where(first, both_up, both_down)

    raw = lax.dot_general(
        every[:, :width], weights, (((1,), (1,)), ((), ())), preferred_element_type=jnp.float32
    )
    hidden = raw.shape[1]
    raw = raw.reshape(columns, 2, tok, hidden)
    own = jnp.where(first, raw[:, 0], raw[:, 1]).reshape(columns * tok, hidden)
    other = jnp.where(first, raw[:, 1], raw[:, 0]).reshape(columns * tok, hidden)
    back = swap(other)
    pre_act = jnp.where(first, own, back)
    hid_grad = jnp.where(first, back, own)
    sig_val = jax.nn.sigmoid(pre_act)
    act_grad = (hid_grad * (sig_val * (1.0 + pre_act * (1.0 - sig_val)))).astype(jnp.bfloat16)
    partial_dg = jnp.sum(hid_grad * (pre_act * sig_val), axis=1)

    tails = every.reshape(columns, 2, tok, -1)[..., width:]
    tails = jnp.where(first, tails[:, 0], tails[:, 1]).reshape(columns * tok, LANES)
    lane = jnp.arange(LANES)
    named = ((lane % EXPERTS == expert) & (lane < 3 * EXPERTS)).astype(jnp.float32)
    weight = jnp.sum(tails.astype(jnp.float32) * named, axis=1)

    partial_dx = jnp.dot(act_grad, both_up, preferred_element_type=jnp.float32) * weight[:, None]
    slot = (lane == expert).astype(jnp.float32)
    packed = jnp.concatenate([partial_dx, partial_dg[:, None] * slot], axis=1)
    packed = packed.reshape(columns, tok, width + LANES)
    summed = lax.psum_scatter(packed, COLUMN, scatter_dimension=0, tiled=True)[0]
    grad_bf = summed[:, :width].astype(jnp.bfloat16)
    token_dg = summed[:, width : width + EXPERTS]
    gate_grad = jnp.sum(onehot * token_dg[:, None, :], axis=2)
    sections = lax.axis_size("pipe")
    handed = lax.ppermute(grad_bf[None], "pipe", [(i, i - 1) for i in range(1, sections)])
    return handed, gate_grad[None]


def solution(mesh):
    pipe, expert = mesh.axis_names
    sections, devices = mesh.devices.shape
    fine = Mesh(
        mesh.devices.reshape(sections, devices // 4, 2, 2), (pipe, "z", "xl", "c")
    )
    inner = ("z", "xl", "c")
    rows = P("pipe", inner, None)
    return jax.shard_map(
        on_device,
        mesh=fine,
        in_specs=(rows, rows, rows, rows, P("pipe", None, inner), rows),
        out_specs=(rows, rows),
        check_vma=False,
    )
```

```python
import jax
import jax.numpy as jnp
from jax import lax
from jax.sharding import Mesh
from jax.sharding import PartitionSpec as P

EXPERTS = 16
LANES = 128
LAG = 2
SPLIT = 4


def swap(block, axis):
    return lax.ppermute(block, axis, [(0, 1), (1, 0)])


def along(block, step, cores=(0, 1)):
    depth = lax.axis_size("z")
    route = []
    for z in range(depth):
        for core in cores:
            to = (z + (step if core == 0 else -step)) % depth
            route.append((2 * z + core, 2 * to + core))
    return lax.ppermute(block, ("z", "c"), route)


def pieces(values):
    high = lax.reduce_precision(values, 8, 7)
    rest = values - high
    middle = lax.reduce_precision(rest, 8, 7)
    return high, middle, rest - middle


def tie(value, *others):
    return lax.optimization_barrier((value, *others))[0]


def on_device(activations, out_grads, gate_vals, routes, up_weight, down_weight):
    inputs, upstream = activations[0], out_grads[0]
    gates, chosen = gate_vals[0], routes[0]
    local_up, local_down = up_weight[0], down_weight[0]
    tok, width = inputs.shape
    first = lax.axis_index("c") == 0
    expert = lax.axis_index("z")
    reach = lax.axis_size("z") // 2
    lane = jnp.arange(LANES)

    onehot = (chosen[:, :, None] == jnp.arange(EXPERTS, dtype=jnp.int32)).astype(jnp.float32)
    dense = jnp.sum(onehot * gates[:, :, None], axis=1)
    tail = jnp.concatenate(pieces(dense), axis=1).astype(jnp.bfloat16)
    tail = jnp.pad(tail, ((0, 0), (0, LANES - tail.shape[1])))
    pack = jnp.stack(
        [
            jnp.concatenate([inputs, tail], axis=1),
            jnp.concatenate([upstream, jnp.zeros_like(tail)], axis=1),
        ]
    )
    got = swap(pack, "c")
    block = jnp.concatenate([jnp.where(first, pack, got), jnp.where(first, got, pack)], axis=1)

    def chip_wide(local, axis):
        other = swap(local, "c")
        return jnp.concatenate(
            [jnp.where(first, local, other), jnp.where(first, other, local)], axis=axis
        )

    wide_up = chip_wide(local_up, 1)
    wide_down = chip_wide(local_down, 0)

    current, near, far = block, [], []
    for step in range(1, reach + 1):
        if step > LAG + 1:
            current = tie(current, far[step - LAG - 2])
        current = along(current, 1, (0, 1) if step < reach else (0,))
        if step == reach:
            current = jnp.where(first, current, block)
        near.append(current)
        far.append(swap(current, "xl"))

    def terms(slots):
        rows_of = lambda part: jnp.concatenate(
            [side[slot][part] for slot in slots for side in (near, far)], axis=0
        )
        in_rows, up_rows = rows_of(0), rows_of(1)
        pre_act = jnp.dot(in_rows[:, :width], wide_up, preferred_element_type=jnp.float32)
        hid_grad = lax.dot_general(
            up_rows[:, :width],
            wide_down,
            (((1,), (1,)), ((), ())),
            preferred_element_type=jnp.float32,
        )
        sig_val = jax.nn.sigmoid(pre_act)
        act_grad = (hid_grad * (sig_val * (1.0 + pre_act * (1.0 - sig_val)))).astype(jnp.bfloat16)
        partial_dg = jnp.sum(hid_grad * (pre_act * sig_val), axis=1, keepdims=True)
        named = ((lane % EXPERTS == expert) & (lane < 3 * EXPERTS)).astype(jnp.float32)
        weight = jnp.sum(in_rows[:, width:].astype(jnp.float32) * named, axis=1, keepdims=True)
        partial_dx = lax.dot_general(
            act_grad, wide_up, (((1,), (1,)), ((), ())), preferred_element_type=jnp.float32
        )
        spread = sum(
            piece * (lane == expert + at * EXPERTS).astype(jnp.float32)
            for at, piece in enumerate(pieces(partial_dg))
        )
        packed = jnp.concatenate([partial_dx * weight, spread], axis=1)
        return packed.reshape(len(slots), 4 * tok, width + LANES)

    parts = list(terms(range(SPLIT))) + list(terms(range(SPLIT, reach)))
    carry = parts[-1]
    for step in range(reach):
        moved = along(carry.astype(jnp.bfloat16), -1, (0, 1) if step else (0,))
        added = parts[reach - 2 - step] if step < reach - 1 else jnp.where(first, 0.0, parts[-1])
        carry = moved.astype(jnp.float32) + added

    carry = carry.reshape(2, 2, tok, width + LANES)
    keep = jnp.where(first, carry[:, 0], carry[:, 1])
    give = jnp.where(first, carry[:, 1], carry[:, 0])
    both = keep + swap(give, "c")
    summed = both[0] + swap(both[1], "xl")
    grad_bf = summed[:, :width].astype(jnp.bfloat16)
    token_dg = sum(summed[:, width + at : width + at + EXPERTS] for at in (0, EXPERTS, 2 * EXPERTS))
    gate_grad = jnp.sum(onehot * token_dg[:, None, :], axis=2)
    sections = lax.axis_size("pipe")
    handed = lax.ppermute(grad_bf[None], "pipe", [(i, i - 1) for i in range(1, sections)])
    return handed, gate_grad[None]


def solution(mesh):
    pipe, expert = mesh.axis_names
    sections, devices = mesh.devices.shape
    fine = Mesh(mesh.devices.reshape(sections, devices // 4, 2, 2), (pipe, "z", "xl", "c"))
    inner = ("z", "xl", "c")
    rows = P("pipe", inner, None)
    return jax.shard_map(
        on_device,
        mesh=fine,
        in_specs=(rows, rows, rows, rows, P("pipe", None, inner), rows),
        out_specs=(rows, rows),
        check_vma=False,
    )
```

```python
import jax
import jax.numpy as jnp
from jax import lax
from jax.sharding import Mesh
from jax.sharding import PartitionSpec as P

EXPERTS = 16
LANES = 128
SEND_FAR = (0, 3, 5)
SEND_NEAR = (1, 2, 2)
PASS_ON = (7, 8, 8)


def swap(block, axis):
    return lax.ppermute(block, axis, [(0, 1), (1, 0)])


def along(block, step, cores=(0, 1)):
    depth = lax.axis_size("z")
    route = []
    for z in range(depth):
        for core in cores:
            to = (z + (step if core == 0 else -step)) % depth
            route.append((2 * z + core, 2 * to + core))
    return lax.ppermute(block, ("z", "c"), route)


def pieces(values):
    high = lax.reduce_precision(values, 8, 7)
    rest = values - high
    middle = lax.reduce_precision(rest, 8, 7)
    return high, middle, rest - middle


def after(value, *others):
    return lax.optimization_barrier((value, *others))[0]


def on_device(activations, out_grads, gate_vals, routes, up_weight, down_weight):
    inputs, upstream = activations[0], out_grads[0]
    gates, chosen = gate_vals[0], routes[0]
    local_up, local_down = up_weight[0], down_weight[0]
    tok, width = inputs.shape
    first = lax.axis_index("c") == 0
    expert = lax.axis_index("z")
    reach = lax.axis_size("z") // 2
    lane = jnp.arange(LANES)

    onehot = (chosen[:, :, None] == jnp.arange(EXPERTS, dtype=jnp.int32)).astype(jnp.float32)
    dense = jnp.sum(onehot * gates[:, :, None], axis=1)
    tail = jnp.concatenate(pieces(dense), axis=1).astype(jnp.bfloat16)
    tail = jnp.pad(tail, ((0, 0), (0, LANES - tail.shape[1])))
    tailed = jnp.concatenate([inputs, tail], axis=1)
    middle = width // 2

    def beside(rows):
        got = swap(rows, "c")
        return jnp.concatenate([jnp.where(first, rows, got), jnp.where(first, got, rows)], axis=0)

    blocks = [beside(tailed), beside(upstream)]

    low_up, high_up = local_up[:middle], local_up[middle:]
    pieces_of = (local_down, low_up, high_up)
    far, other, far_other = [None] * 3, [None] * 3, [None] * 3
    far[0] = swap(local_down, "xl")

    current, kept = blocks, [[], []]
    for step in range(1, reach + 1):
        cores = (0, 1) if step < reach else (0,)
        current = [along(chain, 1, cores) for chain in current]
        for at in range(3):
            if step == SEND_FAR[at]:
                far[at] = swap(after(pieces_of[at], current[0]), "xl")
            if step == SEND_NEAR[at]:
                other[at] = swap(after(pieces_of[at], current[1]), "c")
            if step == PASS_ON[at]:
                far_other[at] = swap(after(far[at], *current), "c")
        if step == reach:
            current = [jnp.where(first, chain, own) for chain, own in zip(current, blocks)]
        for side, chain in zip(kept, current):
            side.append(chain)
    in_rows = jnp.concatenate(kept[0], axis=0)
    up_rows = jnp.concatenate(kept[1], axis=0)

    def dot(left, right, left_dim, right_dim):
        return lax.dot_general(
            left,
            right,
            (((left_dim,), (right_dim,)), ((), ())),
            preferred_element_type=jnp.float32,
        )

    def terms(down_part, low_part, high_part):
        hid_grad = dot(up_rows, down_part, 1, 1)
        pre_act = dot(in_rows[:, :middle], low_part, 1, 0)
        pre_act = pre_act + dot(in_rows[:, middle:width], high_part, 1, 0)
        sig_val = jax.nn.sigmoid(pre_act)
        act_grad = (hid_grad * (sig_val * (1.0 + pre_act * (1.0 - sig_val)))).astype(jnp.bfloat16)
        partial_dg = jnp.sum(hid_grad * (pre_act * sig_val), axis=1, keepdims=True)
        return dot(act_grad, low_part, 1, 1), dot(act_grad, high_part, 1, 1), partial_dg

    found = [terms(*pieces_of), terms(*other)]
    far = [after(part, *found[0], *found[1]) for part in far]
    found.append(terms(*far))
    far_other = [after(part, found[2][2]) for part in far_other]
    found.append(terms(*far_other))
    low_dx, high_dx, token_terms = (sum(column) for column in zip(*found))

    named = ((lane % EXPERTS == expert) & (lane < 3 * EXPERTS)).astype(jnp.float32)
    weight = jnp.sum(in_rows[:, width:].astype(jnp.float32) * named, axis=1, keepdims=True)
    spread = sum(
        piece * (lane == expert + at * EXPERTS).astype(jnp.float32)
        for at, piece in enumerate(pieces(token_terms))
    )
    chains = [low_dx * weight, jnp.concatenate([high_dx * weight, spread], axis=1)]
    chains = [chain.reshape(reach, 2 * tok, chain.shape[1]) for chain in chains]

    carry = [chain[reach - 1] for chain in chains]
    for step in range(reach):
        cores = (0, 1) if step else (0,)
        moved = [along(part.astype(jnp.bfloat16), -1, cores) for part in carry]
        if step < reach - 1:
            added = [chain[reach - 2 - step] for chain in chains]
        else:
            added = [jnp.where(first, 0.0, chain[reach - 1]) for chain in chains]
        carry = [part.astype(jnp.float32) + more for part, more in zip(moved, added)]

    carry = jnp.concatenate(carry, axis=1)
    keep = jnp.where(first, carry[:tok], carry[tok:])
    give = jnp.where(first, carry[tok:], carry[:tok])
    summed = keep + swap(give, "c")
    grad_bf = summed[:, :width].astype(jnp.bfloat16)
    token_dg = sum(summed[:, width + at : width + at + EXPERTS] for at in (0, EXPERTS, 2 * EXPERTS))
    gate_grad = jnp.sum(onehot * token_dg[:, None, :], axis=2)
    sections = lax.axis_size("pipe")
    handed = lax.ppermute(grad_bf[None], "pipe", [(i, i - 1) for i in range(1, sections)])
    return handed, gate_grad[None]


def solution(mesh):
    pipe, expert = mesh.axis_names
    sections, devices = mesh.devices.shape
    fine = Mesh(mesh.devices.reshape(sections, devices // 4, 2, 2), (pipe, "z", "xl", "c"))
    inner = ("z", "xl", "c")
    rows = P("pipe", inner, None)
    return jax.shard_map(
        on_device,
        mesh=fine,
        in_specs=(rows, rows, rows, rows, P("pipe", None, inner), rows),
        out_specs=(rows, rows),
        check_vma=False,
    )
```

```python
import jax
import jax.numpy as jnp
from jax import lax
from jax.sharding import Mesh
from jax.sharding import PartitionSpec as P

EXPERTS = 16
LANES = 128


def swap(block, axis):
    return lax.ppermute(block, axis, [(0, 1), (1, 0)])


def along(block, step, cores=(0, 1)):
    depth = lax.axis_size("z")
    route = []
    for z in range(depth):
        for core in cores:
            to = (z + (step if core == 0 else -step)) % depth
            route.append((2 * z + core, 2 * to + core))
    return lax.ppermute(block, ("z", "c"), route)


def pieces(values):
    high = lax.reduce_precision(values, 8, 7)
    rest = values - high
    middle = lax.reduce_precision(rest, 8, 7)
    return high, middle, rest - middle


def after(value, *others):
    return lax.optimization_barrier((value, *others))[0]


def on_device(activations, out_grads, gate_vals, routes, up_weight, down_weight):
    inputs, upstream = activations[0], out_grads[0]
    gates, chosen = gate_vals[0], routes[0]
    local_up, local_down = up_weight[0], down_weight[0]
    tok, width = inputs.shape
    first = lax.axis_index("c") == 0
    expert = lax.axis_index("z")
    reach = lax.axis_size("z") // 2
    lane = jnp.arange(LANES)

    onehot = (chosen[:, :, None] == jnp.arange(EXPERTS, dtype=jnp.int32)).astype(jnp.float32)
    dense = jnp.sum(onehot * gates[:, :, None], axis=1)
    tail = jnp.concatenate(pieces(dense), axis=1).astype(jnp.bfloat16)
    tail = jnp.pad(tail, ((0, 0), (0, LANES - tail.shape[1])))
    tailed = jnp.concatenate([inputs, tail], axis=1)
    middle = width // 2

    def beside(rows):
        got = swap(rows, "c")
        return jnp.concatenate([jnp.where(first, rows, got), jnp.where(first, got, rows)], axis=0)

    blocks = [beside(tailed), beside(upstream)]

    halves = lambda whole: (whole[:middle], whole[middle:])
    far_down, passed_down = swap(local_down, "xl"), None
    far_up, passed_up = [None, None], [None, None]

    current, kept = blocks, [[], []]
    for step in range(1, reach + 1):
        cores = (0, 1) if step < reach else (0,)
        current = [along(chain, 1, cores) for chain in current]
        lead = current[0]
        if step == 1:
            near_down = swap(after(local_down, lead), "c")
        if step == 2:
            far_up[0] = swap(after(local_up, lead)[:middle], "xl")
        if step == 3:
            near_up = swap(after(local_up, lead), "c")
        if step == 4:
            far_up[1] = swap(after(local_up, lead)[middle:], "xl")
        if step == 6:
            passed_down = swap(after(far_down, lead), "c")
        if step == 7:
            passed_up[0] = swap(after(far_up[0], lead), "c")
        if step == reach:
            passed_up[1] = swap(after(far_up[1], lead, passed_down), "c")
            current = [jnp.where(first, chain, own) for chain, own in zip(current, blocks)]
        for side, chain in zip(kept, current):
            side.append(chain)
    in_rows = jnp.concatenate(kept[0], axis=0)
    up_rows = jnp.concatenate(kept[1], axis=0)

    def dot(left, right, left_dim, right_dim):
        return lax.dot_general(
            left,
            right,
            (((left_dim,), (right_dim,)), ((), ())),
            preferred_element_type=jnp.float32,
        )

    def terms(down_part, low_part, high_part):
        hid_grad = dot(up_rows, down_part, 1, 1)
        pre_act = dot(in_rows[:, :middle], low_part, 1, 0)
        pre_act = pre_act + dot(in_rows[:, middle:width], high_part, 1, 0)
        sig_val = jax.nn.sigmoid(pre_act)
        act_grad = (hid_grad * (sig_val * (1.0 + pre_act * (1.0 - sig_val)))).astype(jnp.bfloat16)
        partial_dg = jnp.sum(hid_grad * (pre_act * sig_val), axis=1, keepdims=True)
        return dot(act_grad, low_part, 1, 1), dot(act_grad, high_part, 1, 1), partial_dg

    found = [terms(local_down, *halves(local_up)), terms(near_down, *halves(near_up))]
    done = (*found[0], *found[1])
    found.append(terms(after(far_down, *done), *[after(part, *done) for part in far_up]))
    found.append(terms(*[after(part, found[2][2]) for part in (passed_down, *passed_up)]))
    low_dx, high_dx, token_terms = (sum(column) for column in zip(*found))

    named = ((lane % EXPERTS == expert) & (lane < 3 * EXPERTS)).astype(jnp.float32)
    weight = jnp.sum(in_rows[:, width:].astype(jnp.float32) * named, axis=1, keepdims=True)
    spread = sum(
        piece * (lane == expert + at * EXPERTS).astype(jnp.float32)
        for at, piece in enumerate(pieces(token_terms))
    )
    packed = jnp.concatenate([low_dx * weight, high_dx * weight, spread], axis=1)
    parts = packed.astype(jnp.bfloat16).reshape(reach, 2 * tok, width + LANES)

    def plus(moved, more):
        return moved.astype(jnp.float32) + more.astype(jnp.float32)

    even, odd = parts[reach - 1], parts[reach - 2]
    for at in range(reach - 3, 0, -2):
        cores = (0, 1) if at < reach - 3 else (0,)
        even = plus(along(even, -2, cores), parts[at]).astype(jnp.bfloat16)
        odd = plus(along(odd, -2), after(parts[at - 1], even)).astype(jnp.bfloat16)
    own = jnp.where(first, 0.0, parts[reach - 1].astype(jnp.float32))
    carry = plus(along(even, -2), along(odd, -1)) + own
    keep = jnp.where(first, carry[:tok], carry[tok:])
    give = jnp.where(first, carry[tok:], carry[:tok])
    summed = keep + swap(give, "c")
    grad_bf = summed[:, :width].astype(jnp.bfloat16)
    token_dg = sum(summed[:, width + at : width + at + EXPERTS] for at in (0, EXPERTS, 2 * EXPERTS))
    gate_grad = jnp.sum(onehot * token_dg[:, None, :], axis=2)
    sections = lax.axis_size("pipe")
    handed = lax.ppermute(grad_bf[None], "pipe", [(i, i - 1) for i in range(1, sections)])
    return handed, gate_grad[None]


def solution(mesh):
    pipe, expert = mesh.axis_names
    sections, devices = mesh.devices.shape
    fine = Mesh(mesh.devices.reshape(sections, devices // 4, 2, 2), (pipe, "z", "xl", "c"))
    inner = ("z", "xl", "c")
    rows = P("pipe", inner, None)
    return jax.shard_map(
        on_device,
        mesh=fine,
        in_specs=(rows, rows, rows, rows, P("pipe", None, inner), rows),
        out_specs=(rows, rows),
        check_vma=False,
    )
```

```python
import jax
import jax.numpy as jnp
from jax import lax
from jax.sharding import Mesh
from jax.sharding import PartitionSpec as P


EXPERTS = 16
LANES = 128


def swap(block, axis):
    return lax.ppermute(block, axis, [(0, 1), (1, 0)])


def along(block, step, cores=(0, 1)):
    depth = lax.axis_size("z")
    route = []
    for z in range(depth):
        for core in cores:
            to = (z + (step if core == 0 else -step)) % depth
            route.append((2 * z + core, 2 * to + core))
    return lax.ppermute(block, ("z", "c"), route)


def pieces(values):
    high = lax.reduce_precision(values, 8, 7)
    rest = values - high
    middle = lax.reduce_precision(rest, 8, 7)
    return high, middle, rest - middle


def after(value, *others):
    return lax.optimization_barrier((value, *others))[0]


def section(activations, out_grads, gate_vals, routes, up_weight, down_weight):
    inputs, upstream = activations[0], out_grads[0]
    gates, chosen = gate_vals[0], routes[0]
    local_up, local_down = up_weight[0], down_weight[0]
    tok, width = inputs.shape
    first = lax.axis_index("c") == 0
    expert = lax.axis_index("z")
    reach = lax.axis_size("z") // 2
    lane = jnp.arange(LANES)

    onehot = (chosen[:, :, None] == jnp.arange(EXPERTS, dtype=jnp.int32)).astype(jnp.float32)
    dense = jnp.sum(onehot * gates[:, :, None], axis=1)
    tail = jnp.concatenate(pieces(dense), axis=1).astype(jnp.bfloat16)
    tail = jnp.pad(tail, ((0, 0), (0, LANES - tail.shape[1])))
    tailed = jnp.concatenate([inputs, tail], axis=1)
    middle = width // 2

    def beside(rows):
        got = swap(rows, "c")
        return jnp.concatenate([jnp.where(first, rows, got), jnp.where(first, got, rows)], axis=0)

    blocks = [beside(tailed), beside(upstream)]

    halves = lambda whole: (whole[:middle], whole[middle:])
    far_up, passed_up = [None, None], [None, None]
    far_down = swap(local_down, "xl")

    current, kept = list(blocks), [[], []]
    for step in range(1, reach + 1):
        cores = (0, 1) if step < reach else (0,)
        for side in range(2):
            current[side] = along(current[side], 1, cores)
        lead = kept[0][-1] if step > 1 else blocks[0]
        if step == 2:
            far_up[0] = swap(after(local_up, lead)[:middle], "xl")
        if step == 3:
            far_up[1] = swap(after(local_up, lead)[middle:], "xl")
        if step == 4:
            near_down = swap(after(local_down, lead), "c")
        if step == 5:
            near_up = swap(after(local_up, lead), "c")
        if step == 7:
            passed_down = swap(after(far_down, lead), "c")
        if step == reach:
            passed_up[0] = swap(after(far_up[0], lead), "c")
            passed_up[1] = swap(after(far_up[1], current[0], passed_down), "c")
            current = [jnp.where(first, chain, own) for chain, own in zip(current, blocks)]
        for side, chain in zip(kept, current):
            side.append(chain)
    in_rows = jnp.concatenate(kept[0], axis=0)
    up_rows = jnp.concatenate(kept[1], axis=0)

    def dot(left, right, left_dim, right_dim):
        return lax.dot_general(
            left,
            right,
            (((left_dim,), (right_dim,)), ((), ())),
            preferred_element_type=jnp.float32,
        )

    def terms(down_part, low_part, high_part):
        hid_grad = dot(up_rows, down_part, 1, 1)
        pre_act = dot(in_rows[:, :middle], low_part, 1, 0)
        pre_act = pre_act + dot(in_rows[:, middle:width], high_part, 1, 0)
        sig_val = jax.nn.sigmoid(pre_act)
        act_grad = (hid_grad * (sig_val * (1.0 + pre_act * (1.0 - sig_val)))).astype(jnp.bfloat16)
        partial_dg = jnp.sum(hid_grad * (pre_act * sig_val), axis=1, keepdims=True)
        return dot(act_grad, low_part, 1, 1), dot(act_grad, high_part, 1, 1), partial_dg

    found = [terms(local_down, *halves(local_up)), terms(near_down, *halves(near_up))]
    done = (*found[0], *found[1])
    found.append(terms(after(far_down, *done), *[after(part, *done) for part in far_up]))
    found.append(terms(*[after(part, found[2][2]) for part in (passed_down, *passed_up)]))
    low_dx, high_dx, token_terms = (sum(column) for column in zip(*found))

    named = ((lane % EXPERTS == expert) & (lane < 3 * EXPERTS)).astype(jnp.float32)
    weight = jnp.sum(in_rows[:, width:].astype(jnp.float32) * named, axis=1, keepdims=True)
    spread = sum(
        piece * (lane == expert + at * EXPERTS).astype(jnp.float32)
        for at, piece in enumerate(pieces(token_terms))
    )
    packed = jnp.concatenate([low_dx * weight, high_dx * weight, spread], axis=1)
    parts = packed.astype(jnp.bfloat16).reshape(reach, 2 * tok, width + LANES)

    def plus(moved, more):
        return moved.astype(jnp.float32) + more.astype(jnp.float32)

    even, odd = parts[reach - 1], parts[reach - 2]
    for at in range(reach - 3, 0, -2):
        cores = (0, 1) if at < reach - 3 else (0,)
        even = plus(along(even, -2, cores), parts[at]).astype(jnp.bfloat16)
        odd = plus(along(odd, -2), after(parts[at - 1], even)).astype(jnp.bfloat16)
    own = jnp.where(first, 0.0, parts[reach - 1].astype(jnp.float32))
    carry = plus(along(even, -2), along(odd, -1)) + own
    keep = jnp.where(first, carry[:tok], carry[tok:])
    give = jnp.where(first, carry[tok:], carry[:tok])
    summed = keep + swap(give, "c")
    grad_bf = summed[:, :width].astype(jnp.bfloat16)
    token_dg = sum(summed[:, width + at : width + at + EXPERTS] for at in (0, EXPERTS, 2 * EXPERTS))
    gate_grad = jnp.sum(onehot * token_dg[:, None, :], axis=2)
    sections = lax.axis_size("pipe")
    handed = lax.ppermute(grad_bf[None], "pipe", [(i, i - 1) for i in range(1, sections)])
    return handed, gate_grad[None]


def solution(mesh):
    pipe, _ = mesh.axis_names
    sections, devices = mesh.devices.shape
    fine = Mesh(mesh.devices.reshape(sections, devices // 4, 2, 2), (pipe, "z", "xl", "c"))
    inner = ("z", "xl", "c")
    rows = P("pipe", inner, None)
    return jax.shard_map(
        section,
        mesh=fine,
        in_specs=(rows, rows, rows, rows, P("pipe", None, inner), rows),
        out_specs=(rows, rows),
        check_vma=False,
    )
```

```python
import jax
import jax.numpy as jnp
from jax import lax
from jax.sharding import Mesh
from jax.sharding import PartitionSpec as P


EXPERTS = 16
LANES = 128


def swap(block, axis):
    return lax.ppermute(block, axis, [(0, 1), (1, 0)])


def along(block, step, cores=(0, 1)):
    depth = lax.axis_size("z")
    route = []
    for z in range(depth):
        for core in cores:
            to = (z + (step if core == 0 else -step)) % depth
            route.append((2 * z + core, 2 * to + core))
    return lax.ppermute(block, ("z", "c"), route)


def pieces(values):
    high = lax.reduce_precision(values, 8, 7)
    rest = values - high
    middle = lax.reduce_precision(rest, 8, 7)
    return high, middle, rest - middle


def after(value, *others):
    return lax.optimization_barrier((value, *others))[0]


def section(activations, out_grads, gate_vals, routes, up_weight, down_weight):
    inputs, upstream = activations[0], out_grads[0]
    gates, chosen = gate_vals[0], routes[0]
    local_up, local_down = up_weight[0], down_weight[0]
    tok, width = inputs.shape
    first = lax.axis_index("c") == 0
    expert = lax.axis_index("z")
    reach = lax.axis_size("z") // 2
    lane = jnp.arange(LANES)

    onehot = (chosen[:, :, None] == jnp.arange(EXPERTS, dtype=jnp.int32)).astype(jnp.float32)
    dense = jnp.sum(onehot * gates[:, :, None], axis=1)
    tail = jnp.concatenate(pieces(dense), axis=1).astype(jnp.bfloat16)
    tail = jnp.pad(tail, ((0, 0), (0, LANES - tail.shape[1])))
    tailed = jnp.concatenate([inputs, tail], axis=1)
    middle = width // 2

    def beside(rows):
        got = swap(rows, "c")
        return jnp.concatenate([jnp.where(first, rows, got), jnp.where(first, got, rows)], axis=0)

    packed_out = beside(upstream)
    packed_in = beside(tailed)
    blocks = [packed_in, packed_out]

    halves = lambda whole: (whole[:middle], whole[middle:])
    far_up, passed_up = [None, None], [None, None]
    far_down = swap(local_down, "xl")

    current, kept = list(blocks), [[], []]
    for step in range(1, reach + 1):
        cores = (0, 1) if step < reach else (0,)
        for side in range(2):
            current[side] = along(current[side], 1, cores)
        lead = kept[0][-1] if step > 1 else blocks[0]
        if step == 2:
            far_up[0] = swap(after(local_up, lead)[:middle], "xl")
        if step == 3:
            far_up[1] = swap(after(local_up, lead)[middle:], "xl")
        if step == 4:
            near_down = swap(after(local_down, lead), "c")
        if step == 5:
            near_up = swap(after(local_up, lead), "c")
        if step == reach:
            passed_down = swap(after(far_down, lead), "c")
            passed_up[0] = swap(after(far_up[0], lead), "c")
            passed_up[1] = swap(after(far_up[1], current[0], passed_down), "c")
            current = [jnp.where(first, chain, own) for chain, own in zip(current, blocks)]
        for side, chain in zip(kept, current):
            side.append(chain)
    in_rows = jnp.concatenate(kept[0], axis=0)
    up_rows = jnp.concatenate(kept[1], axis=0)

    def dot(left, right, left_dim, right_dim):
        return lax.dot_general(
            left,
            right,
            (((left_dim,), (right_dim,)), ((), ())),
            preferred_element_type=jnp.float32,
        )

    def terms(down_part, low_part, high_part):
        hid_grad = dot(up_rows, down_part, 1, 1)
        pre_act = dot(in_rows[:, :middle], low_part, 1, 0)
        pre_act = pre_act + dot(in_rows[:, middle:width], high_part, 1, 0)
        sig_val = jax.nn.sigmoid(pre_act)
        act_grad = (hid_grad * (sig_val * (1.0 + pre_act * (1.0 - sig_val)))).astype(jnp.bfloat16)
        partial_dg = jnp.sum(hid_grad * (pre_act * sig_val), axis=1, keepdims=True)
        return dot(act_grad, low_part, 1, 1), dot(act_grad, high_part, 1, 1), partial_dg

    found = [terms(local_down, *halves(local_up)), terms(near_down, *halves(near_up))]
    done = (*found[0], *found[1])
    found.append(terms(after(far_down, *done), *[after(part, *done) for part in far_up]))
    found.append(terms(*[after(part, found[2][2]) for part in (passed_down, *passed_up)]))
    low_dx, high_dx, token_terms = (sum(column) for column in zip(*found))

    named = ((lane % EXPERTS == expert) & (lane < 3 * EXPERTS)).astype(jnp.float32)
    weight = jnp.sum(in_rows[:, width:].astype(jnp.float32) * named, axis=1, keepdims=True)
    spread = sum(
        piece * (lane == expert + at * EXPERTS).astype(jnp.float32)
        for at, piece in enumerate(pieces(token_terms))
    )
    packed = jnp.concatenate([low_dx * weight, high_dx * weight, spread], axis=1)
    parts = packed.astype(jnp.bfloat16).reshape(reach, 2 * tok, width + LANES)

    def plus(moved, more):
        return moved.astype(jnp.float32) + more.astype(jnp.float32)

    even, odd = parts[reach - 1], parts[reach - 2]
    for at in range(reach - 3, 0, -2):
        cores = (0, 1) if at < reach - 3 else (0,)
        even = plus(along(even, -2, cores), parts[at]).astype(jnp.bfloat16)
        odd = plus(along(odd, -2), after(parts[at - 1], even)).astype(jnp.bfloat16)
    own = jnp.where(first, 0.0, parts[reach - 1].astype(jnp.float32))
    even = along(even, -2)
    odd = along(odd, -1)
    carry = plus(even, odd) + own
    keep = jnp.where(first, carry[:tok], carry[tok:])
    give = jnp.where(first, carry[tok:], carry[:tok])
    summed = keep + swap(give, "c")
    grad_bf = summed[:, :width].astype(jnp.bfloat16)
    token_dg = sum(summed[:, width + at : width + at + EXPERTS] for at in (0, EXPERTS, 2 * EXPERTS))
    gate_grad = jnp.sum(onehot * token_dg[:, None, :], axis=2)
    sections = lax.axis_size("pipe")
    handed = lax.ppermute(grad_bf[None], "pipe", [(i, i - 1) for i in range(1, sections)])
    return handed, gate_grad[None]


def solution(mesh):
    pipe, _ = mesh.axis_names
    sections, devices = mesh.devices.shape
    fine = Mesh(mesh.devices.reshape(sections, devices // 4, 2, 2), (pipe, "z", "xl", "c"))
    inner = ("z", "xl", "c")
    rows = P("pipe", inner, None)
    return jax.shard_map(
        section,
        mesh=fine,
        in_specs=(rows, rows, rows, rows, P("pipe", None, inner), rows),
        out_specs=(rows, rows),
        check_vma=False,
    )
```

```python
import jax
import jax.numpy as jnp
from jax import lax
from jax.sharding import Mesh
from jax.sharding import PartitionSpec as P


EXPERTS = 16
LANES = 128


def swap(block, axis):
    return lax.ppermute(block, axis, [(0, 1), (1, 0)])


def along(block, step, cores=(0, 1)):
    depth = lax.axis_size("z")
    route = []
    for z in range(depth):
        for core in cores:
            to = (z + (step if core == 0 else -step)) % depth
            route.append((2 * z + core, 2 * to + core))
    return lax.ppermute(block, ("z", "c"), route)


def pieces(values):
    high = lax.reduce_precision(values, 8, 7)
    rest = values - high
    middle = lax.reduce_precision(rest, 8, 7)
    return high, middle, rest - middle


def after(value, *others):
    return lax.optimization_barrier((value, *others))[0]


def section(activations, out_grads, gate_vals, routes, up_weight, down_weight):
    inputs, upstream = activations[0], out_grads[0]
    gates, chosen = gate_vals[0], routes[0]
    local_up, local_down = up_weight[0], down_weight[0]
    tok, width = inputs.shape
    first = lax.axis_index("c") == 0
    expert = lax.axis_index("z")
    reach = lax.axis_size("z") // 2
    lane = jnp.arange(LANES)

    onehot = (chosen[:, :, None] == jnp.arange(EXPERTS, dtype=jnp.int32)).astype(jnp.float32)
    dense = jnp.sum(onehot * gates[:, :, None], axis=1)
    tail = jnp.concatenate(pieces(dense), axis=1).astype(jnp.bfloat16)
    tail = jnp.pad(tail, ((0, 0), (0, LANES - tail.shape[1])))
    tailed = jnp.concatenate([inputs, tail], axis=1)
    middle = width // 2

    def beside(rows):
        got = swap(rows, "c")
        return jnp.concatenate([jnp.where(first, rows, got), jnp.where(first, got, rows)], axis=0)

    packed_out = beside(upstream)
    packed_in = beside(tailed)
    blocks = [packed_in, packed_out]

    halves = lambda whole: (whole[:middle], whole[middle:])
    far_up, passed_up = [None, None], [None, None]
    far_down = swap(local_down, "xl")

    current, kept = list(blocks), [[], []]
    for step in range(1, reach + 1):
        cores = (0, 1) if step < reach else (0,)
        for side in range(2):
            current[side] = along(current[side], 1, cores)
        lead = kept[0][-1] if step > 1 else blocks[0]
        if step == 2:
            far_up[0] = swap(after(local_up, lead)[:middle], "xl")
        if step == 3:
            far_up[1] = swap(after(local_up, lead)[middle:], "xl")
        if step == 4:
            near_down = swap(after(local_down, lead), "c")
        if step == 5:
            near_up = swap(after(local_up, lead), "c")
        if step == reach:
            passed_down = swap(after(far_down, lead), "c")
            passed_up[0] = swap(after(far_up[0], lead), "c")
            passed_up[1] = swap(after(far_up[1], current[0]), "c")
            current = [jnp.where(first, chain, own) for chain, own in zip(current, blocks)]
        for side, chain in zip(kept, current):
            side.append(chain)
    early, late = range(reach - 2), range(reach - 2, reach)
    groups = [
        [jnp.concatenate([side[slot] for slot in slots], axis=0) for side in kept]
        for slots in (early, late)
    ]

    def dot(left, right, left_dim, right_dim):
        return lax.dot_general(
            left,
            right,
            (((left_dim,), (right_dim,)), ((), ())),
            preferred_element_type=jnp.float32,
        )

    def terms(group, down_part, low_part, high_part):
        in_rows, up_rows = groups[group]
        hid_grad = dot(up_rows, down_part, 1, 1)
        pre_act = dot(in_rows[:, :middle], low_part, 1, 0)
        pre_act = pre_act + dot(in_rows[:, middle:width], high_part, 1, 0)
        sig_val = jax.nn.sigmoid(pre_act)
        act_grad = (hid_grad * (sig_val * (1.0 + pre_act * (1.0 - sig_val)))).astype(jnp.bfloat16)
        partial_dg = jnp.sum(hid_grad * (pre_act * sig_val), axis=1, keepdims=True)
        return dot(act_grad, low_part, 1, 1), dot(act_grad, high_part, 1, 1), partial_dg

    def weights_after(parts, *others):
        return [after(part, *others) for part in parts]

    own, near = (local_down, *halves(local_up)), (near_down, *halves(near_up))
    found = [[terms(0, *own)], []]
    found[1].append(terms(1, *own))
    found[1].append(terms(1, *near))
    found[0].append(terms(0, *near))
    far = weights_after((far_down, *far_up), *found[1][0], *found[1][1])
    found[1].append(terms(1, *far))
    found[0].append(terms(0, *weights_after(far, found[1][2][2])))
    passed = weights_after((passed_down, *passed_up), found[1][2][2])
    found[1].append(terms(1, *passed))
    found[0].append(terms(0, *weights_after(passed, *found[1][3])))

    named = ((lane % EXPERTS == expert) & (lane < 3 * EXPERTS)).astype(jnp.float32)

    def pack(group):
        low_dx, high_dx, token_terms = (sum(column) for column in zip(*found[group]))
        tails = groups[group][0][:, width:].astype(jnp.float32)
        weight = jnp.sum(tails * named, axis=1, keepdims=True)
        spread = sum(
            piece * (lane == expert + at * EXPERTS).astype(jnp.float32)
            for at, piece in enumerate(pieces(token_terms))
        )
        packed = jnp.concatenate([low_dx * weight, high_dx * weight, spread], axis=1)
        return list(packed.astype(jnp.bfloat16).reshape(-1, 2 * tok, width + LANES))

    parts = pack(0) + pack(1)

    def plus(moved, more):
        return moved.astype(jnp.float32) + more.astype(jnp.float32)

    even, odd = parts[reach - 1], parts[reach - 2]
    for at in range(reach - 3, 0, -2):
        cores = (0, 1) if at < reach - 3 else (0,)
        moved = along(even, -2, cores), along(odd, -2)
        even = plus(moved[0], parts[at]).astype(jnp.bfloat16)
        odd = plus(moved[1], after(parts[at - 1], even)).astype(jnp.bfloat16)
    own = jnp.where(first, 0.0, parts[reach - 1].astype(jnp.float32))
    even = along(even, -2)
    odd = along(odd, -1)
    carry = plus(even, odd) + own
    keep = jnp.where(first, carry[:tok], carry[tok:])
    give = jnp.where(first, carry[tok:], carry[:tok])
    summed = keep + swap(give, "c")
    grad_bf = summed[:, :width].astype(jnp.bfloat16)
    token_dg = sum(summed[:, width + at : width + at + EXPERTS] for at in (0, EXPERTS, 2 * EXPERTS))
    gate_grad = jnp.sum(onehot * token_dg[:, None, :], axis=2)
    sections = lax.axis_size("pipe")
    handed = lax.ppermute(grad_bf[None], "pipe", [(i, i - 1) for i in range(1, sections)])
    return handed, gate_grad[None]


def solution(mesh):
    pipe, _ = mesh.axis_names
    sections, devices = mesh.devices.shape
    fine = Mesh(mesh.devices.reshape(sections, devices // 4, 2, 2), (pipe, "z", "xl", "c"))
    inner = ("z", "xl", "c")
    rows = P("pipe", inner, None)
    return jax.shard_map(
        section,
        mesh=fine,
        in_specs=(rows, rows, rows, rows, P("pipe", None, inner), rows),
        out_specs=(rows, rows),
        check_vma=False,
    )
```

```python
import jax
import jax.numpy as jnp
from jax import lax
from jax.sharding import Mesh
from jax.sharding import PartitionSpec as P


EXPERTS = 16
LANES = 128


def swap(block, axis):
    return lax.ppermute(block, axis, [(0, 1), (1, 0)])


def along(block, step, cores=(0, 1)):
    depth = lax.axis_size("z")
    route = []
    for z in range(depth):
        for core in cores:
            to = (z + (step if core == 0 else -step)) % depth
            route.append((2 * z + core, 2 * to + core))
    return lax.ppermute(block, ("z", "c"), route)


def pieces(values):
    high = lax.reduce_precision(values, 8, 7)
    rest = values - high
    middle = lax.reduce_precision(rest, 8, 7)
    return high, middle, rest - middle


def after(value, *others):
    return lax.optimization_barrier((value, *others))[0]


def section(activations, out_grads, gate_vals, routes, up_weight, down_weight):
    inputs, upstream = activations[0], out_grads[0]
    gates, chosen = gate_vals[0], routes[0]
    local_up, local_down = up_weight[0], down_weight[0]
    tok, width = inputs.shape
    first = lax.axis_index("c") == 0
    expert = lax.axis_index("z")
    reach = lax.axis_size("z") // 2
    lane = jnp.arange(LANES)

    onehot = (chosen[:, :, None] == jnp.arange(EXPERTS, dtype=jnp.int32)).astype(jnp.float32)
    dense = jnp.sum(onehot * gates[:, :, None], axis=1)
    tail = jnp.concatenate(pieces(dense), axis=1).astype(jnp.bfloat16)
    tail = jnp.pad(tail, ((0, 0), (0, LANES - tail.shape[1])))
    tailed = jnp.concatenate([inputs, tail], axis=1)
    middle = width // 2

    def beside(rows):
        got = swap(rows, "c")
        return jnp.concatenate([jnp.where(first, rows, got), jnp.where(first, got, rows)], axis=0)

    packed_out = beside(upstream)
    packed_in = beside(tailed)
    blocks = [packed_in, packed_out]

    halves = lambda whole: (whole[:middle], whole[middle:])
    far_down = swap(local_down, "xl")

    current, kept = list(blocks), [[], []]
    for step in range(1, reach + 1):
        cores = (0, 1) if step < reach else (0,)
        for side in range(2):
            current[side] = along(current[side], 1, cores)
        lead = kept[0][-1] if step > 1 else blocks[0]
        if step == 2:
            far_up = swap(after(local_up, lead), "xl")
        if step == 4:
            near_down = swap(after(local_down, lead), "c")
        if step == 6:
            near_up = swap(after(local_up, lead), "c")
        if step == reach:
            passed_down = swap(after(far_down, lead), "c")
            passed_up = swap(after(far_up, current[0]), "c")
            current = [jnp.where(first, chain, own) for chain, own in zip(current, blocks)]
        for side, chain in zip(kept, current):
            side.append(chain)
    in_rows = jnp.concatenate(kept[0], axis=0)
    up_rows = jnp.concatenate(kept[1], axis=0)

    def dot(left, right, left_dim, right_dim):
        return lax.dot_general(
            left,
            right,
            (((left_dim,), (right_dim,)), ((), ())),
            preferred_element_type=jnp.float32,
        )

    def terms(down_part, low_part, high_part):
        hid_grad = dot(up_rows, down_part, 1, 1)
        pre_act = dot(in_rows[:, :middle], low_part, 1, 0)
        pre_act = pre_act + dot(in_rows[:, middle:width], high_part, 1, 0)
        sig_val = jax.nn.sigmoid(pre_act)
        act_grad = (hid_grad * (sig_val * (1.0 + pre_act * (1.0 - sig_val)))).astype(jnp.bfloat16)
        partial_dg = jnp.sum(hid_grad * (pre_act * sig_val), axis=1, keepdims=True)
        return dot(act_grad, low_part, 1, 1), dot(act_grad, high_part, 1, 1), partial_dg

    found = [terms(local_down, *halves(local_up))]
    found.append(terms(near_down, *halves(near_up)))
    done = (*found[0], *found[1])
    found.append(terms(after(far_down, *done), *halves(after(far_up, *done))))
    last = found[2][2]
    found.append(terms(after(passed_down, last), *halves(after(passed_up, last))))
    low_dx, high_dx, token_terms = (sum(column) for column in zip(*found))

    named = ((lane % EXPERTS == expert) & (lane < 3 * EXPERTS)).astype(jnp.float32)
    weight = jnp.sum(in_rows[:, width:].astype(jnp.float32) * named, axis=1, keepdims=True)
    spread = sum(
        piece * (lane == expert + at * EXPERTS).astype(jnp.float32)
        for at, piece in enumerate(pieces(token_terms))
    )
    packed = jnp.concatenate([low_dx * weight, high_dx * weight, spread], axis=1)
    parts = packed.astype(jnp.bfloat16).reshape(reach, 2 * tok, width + LANES)

    def plus(moved, more):
        return moved.astype(jnp.float32) + more.astype(jnp.float32)

    even, odd = parts[reach - 1], parts[reach - 2]
    for at in range(reach - 3, 0, -2):
        cores = (0, 1) if at < reach - 3 else (0,)
        even = plus(along(even, -2, cores), parts[at]).astype(jnp.bfloat16)
        odd = plus(along(odd, -2), after(parts[at - 1], even)).astype(jnp.bfloat16)
    own = jnp.where(first, 0.0, parts[reach - 1].astype(jnp.float32))
    even = along(even, -2)
    odd = along(odd, -1)
    carry = plus(even, odd) + own
    keep = jnp.where(first, carry[:tok], carry[tok:])
    give = jnp.where(first, carry[tok:], carry[:tok])
    summed = keep + swap(give, "c")
    grad_bf = summed[:, :width].astype(jnp.bfloat16)
    token_dg = sum(summed[:, width + at : width + at + EXPERTS] for at in (0, EXPERTS, 2 * EXPERTS))
    gate_grad = jnp.sum(onehot * token_dg[:, None, :], axis=2)
    sections = lax.axis_size("pipe")
    handed = lax.ppermute(grad_bf[None], "pipe", [(i, i - 1) for i in range(1, sections)])
    return handed, gate_grad[None]


def solution(mesh):
    pipe, _ = mesh.axis_names
    sections, devices = mesh.devices.shape
    fine = Mesh(mesh.devices.reshape(sections, devices // 4, 2, 2), (pipe, "z", "xl", "c"))
    inner = ("z", "xl", "c")
    rows = P("pipe", inner, None)
    return jax.shard_map(
        section,
        mesh=fine,
        in_specs=(rows, rows, rows, rows, P("pipe", None, inner), rows),
        out_specs=(rows, rows),
        check_vma=False,
    )
```
